32 devices in a mesh: ka: 8 (over y, x, core), pb: 4 (over z).
Axes of the slice: x: 2, y: 2, z: 4, core: 2. Of those that a mesh axis runs over, the one named last changes fastest.
Arguments:
- targets: bfloat16 [8, 4, 2, 32768], P('ka'), may hold values from -6 to 6
- partners: bfloat16 [4, 2, 2, 32768], P('pb', None, None, 'ka'), may hold values from -6 to 6
- pair_map: int32 [8, 4], P('ka', 'pb'), may hold values from 0 to 63
- shifts: int32 [8, 4, 3], P('ka', 'pb'), may hold values from 0 to 1
Outputs:
- projector: float32 [8, 8, 2, 32768], P('ka', None, None, 'pb')
The draws below stay inside these ranges and needn't reach their ends.
Inputs may be any that keep to these rules, and one draw needn't show every extreme that they name: d = pair_map[k,q] names the mesh point (d // 16, (d // 4) mod 4, d mod 4).
All inputs are finite; a program needn't handle non-finite values.
Results may differ from the reference program's by a relative error of at most 0.015.
Values may be sent and summed in bfloat16 or wider, within the bound.
A program may use at most 64 MiB of HBM per device.

```python
import jax
import jax.numpy as jnp
from jax import lax

GRID = 32
BANDS = 4
OCC = 2
NK = 8
NQ = 4


def touch_ends(entries, own_key, smallest, largest):
    index_at = [jax.random.randint(jax.random.fold_in(own_key, axis), (), 0, length) for axis, length in enumerate(entries.shape)]
    main_axis = entries.shape.index(max(entries.shape))
    next_to = index_at[:main_axis] + [(index_at[main_axis] + 1) % entries.shape[main_axis]] + index_at[main_axis + 1:]
    return entries.at[tuple(index_at)].set(smallest).at[tuple(next_to)].set(largest)


def shard_levels(rng, dims, pieces, least, top_value):
    gain = 1.0
    for axis_at, blocks in pieces:
        steps = jax.random.uniform(jax.random.fold_in(jax.random.fold_in(rng, 6), axis_at), (blocks,), jnp.float32, least / len(pieces), top_value / len(pieces))
        gain = gain * jnp.repeat(jnp.exp(steps), dims[axis_at] // blocks).reshape((-1,) + (1,) * (len(dims) - 1 - axis_at))
    return gain


def scatter_about(stream_key, shape, scale, limit, split=(), kind=jnp.bfloat16):
    gain = shard_levels(stream_key, shape, split, -0.22, 0.18) if split else 1.0
    values = jax.random.normal(stream_key, shape, jnp.float32) * scale * gain
    return jnp.minimum(jnp.maximum(values, -limit), limit).astype(kind)


def setup_inputs(seed: int = 0) -> dict:
    streams_of = jax.random.split(jax.random.key(seed), 5)
    targets = scatter_about(streams_of[0], (NK, BANDS, 2, GRID**3), 1.0, 6.0, ((0, 8),))
    partners = scatter_about(streams_of[1], (NQ, OCC, 2, GRID**3), 1.0, 6.0, ((0, 4), (3, 8)))
    pair_map = touch_ends(jax.random.randint(streams_of[2], (NK, NQ), 0, 64), jax.random.fold_in(streams_of[2], 1), 0, 63).astype(jnp.int32)
    shifts = touch_ends(jax.random.randint(streams_of[3], (NK, NQ, 3), 0, 2), jax.random.fold_in(streams_of[3], 1), 0, 1).astype(jnp.int32)
    return dict(targets=targets, partners=partners, pair_map=pair_map, shifts=shifts)


KPOINT_SCALING = 2.0
SCREENING_CUTOFF = 0.25
FORMS = ('anbm,pbxym->paxyn', 'anbm,pbxmz->paxnz', 'anbm,pbmyz->panyz')

def dft_tables(length):
    counter = jnp.arange(length, dtype=jnp.int32)
    product = counter[:, None] * counter[None, :] % length
    angles = product.astype(jnp.float32) * (2.0 * jnp.pi / length)
    cos_table = jnp.cos(angles)
    sine_lookup_table = jnp.sin(angles)
    forward = jnp.stack([jnp.stack([cos_table, sine_lookup_table], 1), jnp.stack([-sine_lookup_table, cos_table], 1)], 0)
    inverse = jnp.stack([jnp.stack([cos_table, -sine_lookup_table], 1), jnp.stack([sine_lookup_table, cos_table], 1)], 0)
    return (forward.astype(jnp.bfloat16), inverse.astype(jnp.bfloat16))

def coulomb(offset, shift, length):
    counter = jnp.arange(length, dtype=jnp.int32)
    frequency = ((counter + length // 2) % length - length // 2).astype(jnp.float32)
    lattice = (offset // 16, offset // 4 % 4, offset % 4)
    components = [frequency + shift[axis_id].astype(jnp.float32) + lattice[axis_id].astype(jnp.float32) * 0.25 for axis_id in range(3)]
    squared_magnitude = (components[0] * components[0])[:, None, None] + (components[1] * components[1])[None, :, None] + (components[2] * components[2])[None, None, :]
    return KPOINT_SCALING / (squared_magnitude + SCREENING_CUTOFF)

def rounded(values):
    return lax.optimization_barrier(values.astype(jnp.bfloat16))

def transform(exchange_matrix, blocks, form):
    return jnp.einsum(form, exchange_matrix.astype(jnp.float32), blocks.astype(jnp.float32))

def band_field(target, partners, kernel, forward, inverse, length):
    cells = length ** 3
    part_re = partners[:, 0].astype(jnp.float32)
    part_im = partners[:, 1].astype(jnp.float32)
    targ_re = target[0].astype(jnp.float32)
    targ_im = target[1].astype(jnp.float32)
    density = jnp.stack([part_re * targ_re + part_im * targ_im, part_re * targ_im - part_im * targ_re], 1)
    blocks = rounded(density).reshape(-1, 2, length, length, length)
    blocks = rounded(transform(forward, blocks, FORMS[0]))
    blocks = rounded(transform(forward, blocks, FORMS[1]))
    spectrum = transform(forward, blocks, FORMS[2])
    blocks = rounded(spectrum * kernel)
    blocks = rounded(transform(inverse, blocks, FORMS[2]))
    blocks = rounded(transform(inverse, blocks, FORMS[1]))
    potential = transform(inverse, blocks, FORMS[0]).reshape(-1, 2, cells) * (1.0 / cells)
    pot_re = potential[:, 0]
    pot_im = potential[:, 1]
    return -jnp.stack([jnp.sum(part_re * pot_re - part_im * pot_im, 0), jnp.sum(part_re * pot_im + part_im * pot_re, 0)], 0)

def real_vectors(fields):
    real_part = fields[:, 0]
    imag_part = fields[:, 1]
    return jnp.concatenate([jnp.concatenate([real_part, imag_part], 1), jnp.concatenate([-imag_part, real_part], 1)], 0)

def projector_of(target_set, summed, cells):
    basis_set = real_vectors(target_set.astype(jnp.float32))
    images = real_vectors(summed)
    intersection = jnp.dot(basis_set, images.T, precision=lax.Precision.HIGHEST) * (1.0 / cells)
    exchange_matrix = -0.5 * (intersection + intersection.T)
    prefactor_value = jnp.linalg.cholesky(exchange_matrix)
    solved = lax.linalg.triangular_solve(prefactor_value, images, left_side=True, lower=True)
    return solved.reshape(images.shape[0], 2, summed.shape[2])

def reference(targets, partners, pair_map, shifts):
    length = GRID
    cells = length ** 3
    forward, inverse = dft_tables(length)

    def one_target(k_row):
        target_set = targets[k_row]

        def append_partner_orbital(summed, q_row):
            kernel = coulomb(pair_map[k_row, q_row], shifts[k_row, q_row], length)
            occupied_orbitals = partners[q_row]
            fields = lax.map(lambda orbital: band_field(orbital, occupied_orbitals, kernel, forward, inverse, length), target_set)
            return (summed + fields, None)
        summed, unused = lax.scan(append_partner_orbital, jnp.zeros(target_set.shape, jnp.float32), jnp.arange(NQ, dtype=jnp.int32))
        return projector_of(target_set, summed, cells)
    return lax.map(one_target, jnp.arange(NK, dtype=jnp.int32))
```

```python
import functools

import jax
import jax.numpy as jnp
import numpy as np
from jax import lax
from jax.experimental import pallas as pl
from jax.experimental.pallas import tpu as pltpu
from jax.sharding import PartitionSpec as P

GRID = 32
KPOINT_SCALING = 2.0
SCREENING_CUTOFF = 0.25
LANES = 128
MESH = pl.DeviceIdType.MESH
F32 = jnp.float32
BF16 = jnp.bfloat16


def tables(length, group):
    n = np.arange(length)
    angle = (n[:, None] * n[None, :] % length) * (2.0 * np.pi / length)
    eye = np.eye(group)
    c = np.kron(eye, np.cos(angle))
    s = np.kron(eye, np.sin(angle))
    fwd = np.block([[c, -s], [s, c]])
    inv = np.block([[c, s], [-s, c]])
    right = np.stack([fwd, inv])
    left = np.stack([fwd.T, inv.T])
    sel = np.zeros((group, group, length, group, group, length))
    spread = np.zeros((group, length, group, group, length))
    for a in range(group):
        for b in range(group):
            for z in range(length):
                sel[a, b, z, b, a, z] = 1.0
                spread[b, z, b, a, z] = 1.0
    wide = group * group * length
    sel = sel.reshape(wide, wide)
    spread = spread.reshape(group * length, wide)
    return tuple(jnp.asarray(v.astype(BF16)) for v in (right, left, sel, spread))


def dot(a, b):
    return jnp.dot(a, b, preferred_element_type=F32)


def body(
    n_ka, n_pb, pm_ref, sh_ref, t_ref, p_ref, right_ref, left_ref, sel_ref, spread_ref, out_ref,
    gat, t_s, p_s, s, fld, fbf, rcv, ab_snd, ab_rcv, img,
    g_send, g_recv, f_send, f_recv, a_send, a_recv,
):
    L = GRID
    group = LANES // L
    plane = L * L
    share = plane // n_pb
    block = group * L
    n_blocks = plane // block
    ka = lax.axis_index("ka")
    pb = lax.axis_index("pb")

    barrier = pltpu.get_barrier_semaphore()
    for d in range(1, n_ka):
        pl.semaphore_signal(
            barrier, inc=1, device_id={"ka": lax.rem(ka + d, n_ka), "pb": pb}, device_id_type=MESH
        )
    for d in range(1, n_pb):
        pl.semaphore_signal(
            barrier, inc=1, device_id={"ka": ka, "pb": lax.rem(pb + d, n_pb)}, device_id_type=MESH
        )
    pl.semaphore_wait(barrier, n_ka + n_pb - 2)

    gathers = []
    for d in range(1, n_ka):
        copy = pltpu.make_async_remote_copy(
            src_ref=p_ref,
            dst_ref=gat.at[ka],
            send_sem=g_send.at[d - 1],
            recv_sem=g_recv.at[d - 1],
            device_id={"ka": lax.rem(ka + d, n_ka), "pb": pb},
            device_id_type=MESH,
        )
        copy.start()
        gathers.append(copy)
    gat[ka] = p_ref[...]

    for c in range(2):
        wide = jnp.concatenate([t_ref[i, c] for i in range(group)], axis=1)
        turned = dot(wide, sel_ref[...])
        for y in range(group):
            t_s[c, pl.ds(y, plane // group, stride=group), :] = turned[:, y * LANES : (y + 1) * LANES]

    xs = L // n_ka
    part_rows = xs * L // group

    def spread_part(d):
        for j in range(2):
            for c in range(2):
                rows = dot(gat[d, j, c], spread_ref[...])
                for y in range(group):
                    p_s[j, c, pl.ds(d * xs * L + y, part_rows, stride=group), :] = rows[
                        :, y * LANES : (y + 1) * LANES
                    ]

    def forward_block(g):
        rows = pl.ds(pl.multiple_of(g * block, block), block)
        tr = t_s[0, rows, :]
        ti = t_s[1, rows, :]
        dens = []
        for j in range(2):
            pr = p_s[j, 0, rows, :]
            pi = p_s[j, 1, rows, :]
            dens.append(
                jnp.concatenate(
                    [(pr * tr + pi * ti).astype(BF16), (pr * ti - pi * tr).astype(BF16)], axis=1
                )
            )
        along_z = dot(jnp.concatenate(dens, axis=0), right_ref[0]).astype(BF16)
        stacked = jnp.concatenate(
            [
                jnp.concatenate([along_z[:block, :LANES], along_z[block:, :LANES]], axis=1),
                jnp.concatenate([along_z[:block, LANES:], along_z[block:, LANES:]], axis=1),
            ],
            axis=0,
        )
        along_y = dot(left_ref[0], stacked)
        for c in range(2):
            for j in range(2):
                s[c, j, rows, :] = along_y[c * block : (c + 1) * block, j * LANES : (j + 1) * LANES]

    if xs % group == 0:
        per = xs // group
        for d in range(n_ka):
            if d:
                gathers[d - 1].wait_recv()
            owner = lax.rem(ka + n_ka - d, n_ka)
            spread_part(owner)
            for g in range(per):
                forward_block(owner * per + g)
    else:
        for copy in gathers:
            copy.wait_recv()
        for d in range(n_ka):
            spread_part(d)
        lax.fori_loop(0, n_blocks, lambda g, _: (forward_block(g), 0)[1], 0)

    d = pm_ref[0, 0]
    lattice = (d // 16, d // 4 % 4, d % 4)
    offs = [sh_ref[0, a].astype(F32) + lattice[a].astype(F32) * 0.25 for a in range(3)]

    def freq(index, a):
        return (lax.rem(index + L // 2, L) - L // 2).astype(F32) + offs[a]

    row = lax.broadcasted_iota(jnp.int32, (block, LANES), 0)
    lane = lax.broadcasted_iota(jnp.int32, (block, LANES), 1)
    fx = freq(lax.rem(row, L), 0)
    fz = freq(lax.rem(lane, L), 2)
    fx = fx * fx
    fz = fz * fz

    def middle(h, carry):
        fy = freq(h * group + row // L, 1)
        kern = (-KPOINT_SCALING / (L * L * L)) / (fx + fy * fy + fz + SCREENING_CUTOFF)
        stacked = jnp.concatenate(
            [
                jnp.concatenate(
                    [s[c, j, pl.ds(h * group + y, L, stride=L), :].astype(BF16) for j in range(2)], axis=1
                )
                for c in range(2)
                for y in range(group)
            ],
            axis=0,
        )
        spec = dot(left_ref[0], stacked)
        kk = jnp.concatenate([jnp.concatenate([kern, kern], axis=1)] * 2, axis=0)
        back = dot(left_ref[1], (spec * kk).astype(BF16))
        for c in range(2):
            for y in range(group):
                at = c * block + y * L
                for j in range(2):
                    s[c, j, pl.ds(h * group + y, L, stride=L), :] = back[
                        at : at + L, j * LANES : (j + 1) * LANES
                    ]
        return carry

    for h in range(n_blocks):
        middle(h, 0)

    def inverse_block(g):
        rows = pl.ds(pl.multiple_of(g * block, block), block)
        stacked = jnp.concatenate(
            [
                jnp.concatenate([s[c, j, rows, :].astype(BF16) for j in range(2)], axis=1)
                for c in range(2)
            ],
            axis=0,
        )
        back_y = dot(left_ref[1], stacked).astype(BF16)
        turned = jnp.concatenate(
            [
                jnp.concatenate(
                    [back_y[:block, j * LANES : (j + 1) * LANES], back_y[block:, j * LANES : (j + 1) * LANES]],
                    axis=1,
                )
                for j in range(2)
            ],
            axis=0,
        )
        pot = dot(turned, right_ref[1])
        fr = jnp.zeros((block, LANES), F32)
        fi = jnp.zeros((block, LANES), F32)
        for j in range(2):
            pr = p_s[j, 0, rows, :]
            pi = p_s[j, 1, rows, :]
            vr = pot[j * block : (j + 1) * block, :LANES]
            vi = pot[j * block : (j + 1) * block, LANES:]
            fr = fr + (pr * vr - pi * vi)
            fi = fi + (pr * vi + pi * vr)
        fld[0, rows, :] = fr
        fld[1, rows, :] = fi
        hr = fr.astype(BF16)
        hi = fi.astype(BF16)
        fbf[0, rows, :] = hr
        fbf[1, rows, :] = hi
        high = jnp.concatenate([hr, hi], axis=1)
        low = jnp.concatenate(
            [(fr - hr.astype(F32)).astype(BF16), (fi - hi.astype(F32)).astype(BF16)], axis=1
        )
        basis = jnp.concatenate([t_s[0, rows, :].astype(BF16), t_s[1, rows, :].astype(BF16)], axis=1)
        dims = (((0,), (0,)), ((), ()))
        return lax.dot_general(basis, high, dims, preferred_element_type=F32) + lax.dot_general(
            basis, low, dims, preferred_element_type=F32
        )

    gram = jnp.zeros((2 * LANES, 2 * LANES), F32)
    order = sorted(range(1, n_pb), key=lambda v: -min(v, n_pb - v))
    split = share % block == 0
    if not split:
        gram = lax.fori_loop(0, n_blocks, lambda g, acc: acc + inverse_block(g), gram)
    sends = {}
    for d in order + [0]:
        to = lax.rem(pb + d, n_pb)
        if split:
            for g in range(share // block):
                gram = gram + inverse_block(to * (share // block) + g)
        if d:
            copy = pltpu.make_async_remote_copy(
                src_ref=fbf.at[:, pl.ds(pl.multiple_of(to * share, share), share), :],
                dst_ref=rcv.at[d - 1],
                send_sem=f_send.at[d - 1],
                recv_sem=f_recv.at[d - 1],
                device_id={"ka": ka, "pb": to},
                device_id_type=MESH,
            )
            copy.start()
            sends[d] = copy

    same = gram[:LANES, :LANES] + gram[LANES:, LANES:]
    cross = gram[:LANES, LANES:] - gram[LANES:, :LANES]
    keep = lax.rem(row, L) == lax.rem(lane, L)
    same = jnp.where(keep, same, 0.0)
    cross = jnp.where(keep, cross, 0.0)
    same = same + same.T
    cross = cross - cross.T
    ab = jnp.concatenate(
        [jnp.sum(v[i * L : (i + 1) * L], axis=0, keepdims=True) for v in (same, cross) for i in range(group)],
        axis=0,
    )
    ab_snd[...] = ab
    swaps = {}
    for d in order:
        copy = pltpu.make_async_remote_copy(
            src_ref=ab_snd,
            dst_ref=ab_rcv.at[d - 1],
            send_sem=a_send.at[d - 1],
            recv_sem=a_recv.at[d - 1],
            device_id={"ka": ka, "pb": lax.rem(pb + d, n_pb)},
            device_id_type=MESH,
        )
        copy.start()
        swaps[d] = copy

    own = pl.multiple_of(pb * share, share)
    for d in order:
        sends[d].wait_recv()
    for c in range(2):
        total = fld[c, pl.ds(own, share), :]
        for d in order:
            total = total + rcv[d - 1, c].astype(F32)
        fld[c, pl.ds(own, share), :] = total
    quarter = share // group
    lane_q = lax.broadcasted_iota(jnp.int32, (quarter, LANES), 1) // L
    for c in range(2):
        rows = [fld[c, pl.ds(own + y, quarter, stride=group), :] for y in range(group)]
        for k in range(group):
            turned = jnp.zeros((quarter, LANES), F32)
            for y in range(group):
                shift = (y - k) % group * L
                moved = pltpu.roll(rows[y], shift, 1) if shift else rows[y]
                turned = jnp.where(lane_q == y, moved, turned)
            img[k, c] = turned

    for d in order:
        swaps[d].wait_recv()
        ab = ab + ab_rcv[d - 1]
    ab = ab * (-0.5 / (L * L * L))
    n = 2 * group
    sub = lax.broadcasted_iota(jnp.int32, (n, LANES), 0)
    lan = lax.broadcasted_iota(jnp.int32, (n, LANES), 1)
    other = jnp.concatenate([-ab[group:], ab[:group]], axis=0)
    mat = jnp.where(lan == sub + n, 1.0, 0.0).astype(F32)
    for k in range(group):
        a = jnp.sum(jnp.where(lan // L == k, ab, 0.0), axis=1, keepdims=True)
        b = jnp.sum(jnp.where(lan // L == k, other, 0.0), axis=1, keepdims=True)
        mat = jnp.where(lan == k, a, mat)
        mat = jnp.where(lan == group + k, b, mat)
    for k in range(n - 1):
        col = jnp.broadcast_to(mat[:, k : k + 1], (n, LANES))
        ratio = col / col[k : k + 1, :]
        mat = mat - jnp.where(sub > k, ratio, 0.0) * mat[k : k + 1, :]
    diag = jnp.sum(jnp.where(lan == sub, mat, 0.0), axis=1, keepdims=True)
    mat = mat / jnp.sqrt(diag)
    cols = [jnp.broadcast_to(mat[:, n + k : n + k + 1], (n, LANES)) for k in range(n)]
    for r in range(n):
        w = [col[r : r + 1, :] for col in cols]
        re = jnp.zeros((quarter, LANES), F32)
        im = jnp.zeros((quarter, LANES), F32)
        for k in range(group):
            re = re + w[k] * img[k, 0] - w[group + k] * img[k, 1]
            im = im + w[k] * img[k, 1] + w[group + k] * img[k, 0]
        out_ref[r, 0] = re
        out_ref[r, 1] = im

    for copy in gathers:
        copy.wait_send()
    for d in order:
        sends[d].wait_send()
        swaps[d].wait_send()


def local(n_ka, n_pb, targets, partners, pair_map, shifts):
    L = GRID
    plane = L * L
    bands = targets.shape[1]
    occ = partners.shape[1]
    share = plane // n_pb
    group = LANES // L
    t = targets[0].reshape(bands, 2, plane // group, LANES)
    p = partners[0].reshape(occ, 2, -1, LANES)
    consts = tables(L, group)
    vmem = pl.BlockSpec(memory_space=pltpu.VMEM)
    smem = pl.BlockSpec(memory_space=pltpu.SMEM)
    dma = pltpu.SemaphoreType.DMA
    out = pl.pallas_call(
        functools.partial(body, n_ka, n_pb),
        out_shape=jax.ShapeDtypeStruct((2 * bands, 2, share // group, LANES), F32),
        in_specs=[smem, smem] + [vmem] * 6,
        out_specs=vmem,
        scratch_shapes=[
            pltpu.VMEM((n_ka,) + p.shape, BF16),
            pltpu.VMEM((2, plane, LANES), F32),
            pltpu.VMEM((occ, 2, plane, LANES), F32),
            pltpu.VMEM((2, occ, plane, LANES), F32),
            pltpu.VMEM((2, plane, LANES), F32),
            pltpu.VMEM((2, plane, LANES), BF16),
            pltpu.VMEM((n_pb - 1, 2, share, LANES), BF16),
            pltpu.VMEM((2 * bands, LANES), F32),
            pltpu.VMEM((n_pb - 1, 2 * bands, LANES), F32),
            pltpu.VMEM((bands, 2, share // group, LANES), F32),
            dma((n_ka - 1,)),
            dma((n_ka - 1,)),
            dma((n_pb - 1,)),
            dma((n_pb - 1,)),
            dma((n_pb - 1,)),
            dma((n_pb - 1,)),
        ],
        compiler_params=pltpu.CompilerParams(collective_id=0, has_side_effects=True),
    )(pair_map, shifts[0], t, p, *consts)
    return out.reshape(1, 2 * bands, 2, share * L)


def solution(mesh):
    return jax.shard_map(
        functools.partial(local, mesh.shape["ka"], mesh.shape["pb"]),
        mesh=mesh,
        in_specs=(
            P("ka", None, None, None),
            P("pb", None, None, "ka"),
            P("ka", "pb"),
            P("ka", "pb", None),
        ),
        out_specs=P("ka", None, None, "pb"),
        check_vma=False,
    )
```

```python
import functools

import jax
import jax.numpy as jnp
import numpy as np
from jax import lax
from jax.experimental import pallas as pl
from jax.experimental.pallas import tpu as pltpu
from jax.sharding import PartitionSpec as P

GRID = 32
KPOINT_SCALING = 2.0
SCREENING_CUTOFF = 0.25
LANES = 128
MESH = pl.DeviceIdType.MESH
F32 = jnp.float32
BF16 = jnp.bfloat16


def tables(length, group):
    n = np.arange(length)
    angle = (n[:, None] * n[None, :] % length) * (2.0 * np.pi / length)
    eye = np.eye(group)
    c = np.kron(eye, np.cos(angle))
    s = np.kron(eye, np.sin(angle))
    fwd = np.block([[c, -s], [s, c]])
    inv = np.block([[c, s], [-s, c]])
    right = np.stack([fwd, inv])
    plain = np.arange(group * length).reshape(group, length)
    turned = plain.reshape(group, length // group, group).transpose(1, 2, 0).ravel()
    mixed = plain.reshape(group, length // group, group).transpose(1, 0, 2).ravel()
    turned = np.concatenate([turned, turned + group * length])
    mixed = np.concatenate([mixed, mixed + group * length])
    left = np.stack([
        fwd.T[turned], fwd.T[mixed][:, mixed], inv.T[mixed][:, mixed], inv.T[:, turned]
    ])
    sel = np.zeros((group, group, length, group, group, length))
    spread = np.zeros((group, length, group, group, length))
    for a in range(group):
        for b in range(group):
            for z in range(length):
                sel[a, b, z, b, a, z] = 1.0
                spread[b, z, b, a, z] = 1.0
    wide = group * group * length
    sel = sel.reshape(wide, wide)
    spread = spread.reshape(group * length, wide)
    return tuple(jnp.asarray(v.astype(BF16)) for v in (right, left, sel, spread))


def dot(a, b):
    return jnp.dot(a, b, preferred_element_type=F32)


def body(
    n_ka, n_pb, pm_ref, sh_ref, t_ref, p_ref, right_ref, left_ref, sel_ref, spread_ref, out_ref,
    gat, t_de, p_de, t_s, p_s, s, fld, fbf, rcv, ab_snd, ab_rcv, img,
    g_send, g_recv, f_send, f_recv, a_send, a_recv,
):
    L = GRID
    group = LANES // L
    plane = L * L
    share = plane // n_pb
    block = group * L
    n_blocks = plane // block
    ka = lax.axis_index("ka")
    pb = lax.axis_index("pb")

    barrier = pltpu.get_barrier_semaphore()
    for d in range(1, n_ka):
        pl.semaphore_signal(
            barrier, inc=1, device_id={"ka": lax.rem(ka + d, n_ka), "pb": pb}, device_id_type=MESH
        )
    for d in range(1, n_pb):
        pl.semaphore_signal(
            barrier, inc=1, device_id={"ka": ka, "pb": lax.rem(pb + d, n_pb)}, device_id_type=MESH
        )
    pl.semaphore_wait(barrier, n_ka + n_pb - 2)

    gathers = []
    for d in range(1, n_ka):
        copy = pltpu.make_async_remote_copy(
            src_ref=p_ref,
            dst_ref=gat.at[ka],
            send_sem=g_send.at[d - 1],
            recv_sem=g_recv.at[d - 1],
            device_id={"ka": lax.rem(ka + d, n_ka), "pb": pb},
            device_id_type=MESH,
        )
        copy.start()
        gathers.append(copy)
    gat[ka] = p_ref[...]

    t_de[...] = t_ref[...].astype(F32)
    for c in range(2):
        wide = jnp.concatenate(
            [t_de[i, pl.ds(c, plane // group, stride=2), :].astype(BF16) for i in range(group)], axis=1
        )
        turned = dot(wide, sel_ref[...])
        for y in range(group):
            t_s[c, pl.ds(y, plane // group, stride=group), :] = turned[:, y * LANES : (y + 1) * LANES]

    xs = L // n_ka
    part_rows = xs * L // group

    def spread_part(d):
        for j in range(2):
            p_de[j] = gat[d, j].astype(F32)
            for c in range(2):
                rows = dot(p_de[j, pl.ds(c, part_rows, stride=2), :].astype(BF16), spread_ref[...])
                for y in range(group):
                    p_s[j, c, pl.ds(d * xs * L + y, part_rows, stride=group), :] = rows[
                        :, y * LANES : (y + 1) * LANES
                    ]

    def forward_block(g):
        rows = pl.ds(pl.multiple_of(g * block, block), block)
        tr = t_s[0, rows, :]
        ti = t_s[1, rows, :]
        dens = []
        for j in range(2):
            pr = p_s[j, 0, rows, :]
            pi = p_s[j, 1, rows, :]
            dens.append(
                jnp.concatenate(
                    [(pr * tr + pi * ti).astype(BF16), (pr * ti - pi * tr).astype(BF16)], axis=1
                )
            )
        along_z = dot(jnp.concatenate(dens, axis=0), right_ref[0]).astype(BF16)
        stacked = jnp.concatenate(
            [
                jnp.concatenate([along_z[:block, :LANES], along_z[block:, :LANES]], axis=1),
                jnp.concatenate([along_z[:block, LANES:], along_z[block:, LANES:]], axis=1),
            ],
            axis=0,
        )
        along_y = dot(left_ref[0], stacked)
        for c in range(2):
            for j in range(2):
                s[c, j, rows, :] = along_y[
                    c * block : (c + 1) * block, j * LANES : (j + 1) * LANES
                ].astype(BF16)

    if xs % group == 0:
        per = xs // group
        for d in range(n_ka):
            if d:
                gathers[d - 1].wait_recv()
            owner = lax.rem(ka + n_ka - d, n_ka)
            spread_part(owner)
            for g in range(per):
                forward_block(owner * per + g)
    else:
        for copy in gathers:
            copy.wait_recv()
        for d in range(n_ka):
            spread_part(d)
        lax.fori_loop(0, n_blocks, lambda g, _: (forward_block(g), 0)[1], 0)

    d = pm_ref[0, 0]
    lattice = (d // 16, d // 4 % 4, d % 4)
    offs = [sh_ref[0, a].astype(F32) + lattice[a].astype(F32) * 0.25 for a in range(3)]

    def freq(index, a):
        return (lax.rem(index + L // 2, L) - L // 2).astype(F32) + offs[a]

    row = lax.broadcasted_iota(jnp.int32, (block, LANES), 0)
    lane = lax.broadcasted_iota(jnp.int32, (block, LANES), 1)
    tile = group * group
    fx = freq(row // tile * group + lax.rem(row, group), 0)
    fz = freq(lax.rem(lane, L), 2)
    fxz = fx * fx + fz * fz + SCREENING_CUTOFF
    y_lo = lax.rem(row // group, group)

    for h in range(L // group):
        fy = freq(h * group + y_lo, 1)
        kern = (-KPOINT_SCALING / (L * L * L)) / (fxz + fy * fy)
        stacked = jnp.concatenate(
            [
                jnp.concatenate(
                    [s[c, j, g * block + h * tile : g * block + (h + 1) * tile, :] for j in range(2)], axis=1
                )
                for c in range(2)
                for g in range(n_blocks)
            ],
            axis=0,
        )
        spec = dot(left_ref[1], stacked)
        kk = jnp.concatenate([jnp.concatenate([kern, kern], axis=1)] * 2, axis=0)
        back = dot(left_ref[2], (spec * kk).astype(BF16)).astype(BF16)
        for c in range(2):
            for g in range(n_blocks):
                at = c * block + g * tile
                for j in range(2):
                    s[c, j, g * block + h * tile : g * block + (h + 1) * tile, :] = back[
                        at : at + tile, j * LANES : (j + 1) * LANES
                    ]

    def inverse_block(g):
        rows = pl.ds(pl.multiple_of(g * block, block), block)
        stacked = jnp.concatenate(
            [
                jnp.concatenate([s[c, j, rows, :] for j in range(2)], axis=1)
                for c in range(2)
            ],
            axis=0,
        )
        back_y = dot(left_ref[3], stacked).astype(BF16)
        turned = jnp.concatenate(
            [
                jnp.concatenate(
                    [back_y[:block, j * LANES : (j + 1) * LANES], back_y[block:, j * LANES : (j + 1) * LANES]],
                    axis=1,
                )
                for j in range(2)
            ],
            axis=0,
        )
        pot = dot(turned, right_ref[1])
        fr = jnp.zeros((block, LANES), F32)
        fi = jnp.zeros((block, LANES), F32)
        for j in range(2):
            pr = p_s[j, 0, rows, :]
            pi = p_s[j, 1, rows, :]
            vr = pot[j * block : (j + 1) * block, :LANES]
            vi = pot[j * block : (j + 1) * block, LANES:]
            fr = fr + (pr * vr - pi * vi)
            fi = fi + (pr * vi + pi * vr)
        fld[0, rows, :] = fr
        fld[1, rows, :] = fi
        hr = fr.astype(BF16)
        hi = fi.astype(BF16)
        fbf[0, rows, :] = hr
        fbf[1, rows, :] = hi
        high = jnp.concatenate([hr, hi], axis=1)
        low = jnp.concatenate(
            [(fr - hr.astype(F32)).astype(BF16), (fi - hi.astype(F32)).astype(BF16)], axis=1
        )
        basis = jnp.concatenate([t_s[0, rows, :].astype(BF16), t_s[1, rows, :].astype(BF16)], axis=1)
        dims = (((0,), (0,)), ((), ()))
        return lax.dot_general(basis, high, dims, preferred_element_type=F32) + lax.dot_general(
            basis, low, dims, preferred_element_type=F32
        )

    gram = jnp.zeros((2 * LANES, 2 * LANES), F32)
    order = sorted(range(1, n_pb), key=lambda v: -min(v, n_pb - v))
    split = share % block == 0
    if not split:
        gram = lax.fori_loop(0, n_blocks, lambda g, acc: acc + inverse_block(g), gram)
    sends = {}
    for d in order + [0]:
        to = lax.rem(pb + d, n_pb)
        if split:
            for g in range(share // block):
                gram = gram + inverse_block(to * (share // block) + g)
        if d:
            copy = pltpu.make_async_remote_copy(
                src_ref=fbf.at[:, pl.ds(pl.multiple_of(to * share, share), share), :],
                dst_ref=rcv.at[d - 1],
                send_sem=f_send.at[d - 1],
                recv_sem=f_recv.at[d - 1],
                device_id={"ka": ka, "pb": to},
                device_id_type=MESH,
            )
            copy.start()
            sends[d] = copy

    same = gram[:LANES, :LANES] + gram[LANES:, LANES:]
    cross = gram[:LANES, LANES:] - gram[LANES:, :LANES]
    keep = lax.rem(row, L) == lax.rem(lane, L)
    same = jnp.where(keep, same, 0.0)
    cross = jnp.where(keep, cross, 0.0)
    same = same + same.T
    cross = cross - cross.T
    ab = jnp.concatenate(
        [jnp.sum(v[i * L : (i + 1) * L], axis=0, keepdims=True) for v in (same, cross) for i in range(group)],
        axis=0,
    )
    ab_snd[...] = ab
    swaps = {}
    for d in order:
        copy = pltpu.make_async_remote_copy(
            src_ref=ab_snd,
            dst_ref=ab_rcv.at[d - 1],
            send_sem=a_send.at[d - 1],
            recv_sem=a_recv.at[d - 1],
            device_id={"ka": ka, "pb": lax.rem(pb + d, n_pb)},
            device_id_type=MESH,
        )
        copy.start()
        swaps[d] = copy

    own = pl.multiple_of(pb * share, share)
    for d in order:
        sends[d].wait_recv()
    for c in range(2):
        total = fld[c, pl.ds(own, share), :]
        for d in order:
            total = total + rcv[d - 1, c].astype(F32)
        fld[c, pl.ds(own, share), :] = total
    quarter = share // group
    lane_q = lax.broadcasted_iota(jnp.int32, (quarter, LANES), 1) // L
    for c in range(2):
        rows = [fld[c, pl.ds(own + y, quarter, stride=group), :] for y in range(group)]
        for k in range(group):
            turned = jnp.zeros((quarter, LANES), F32)
            for y in range(group):
                shift = (y - k) % group * L
                moved = pltpu.roll(rows[y], shift, 1) if shift else rows[y]
                turned = jnp.where(lane_q == y, moved, turned)
            img[k, c] = turned

    for d in order:
        swaps[d].wait_recv()
        ab = ab + ab_rcv[d - 1]
    ab = ab * (-0.5 / (L * L * L))
    n = 2 * group
    sub = lax.broadcasted_iota(jnp.int32, (n, LANES), 0)
    lan = lax.broadcasted_iota(jnp.int32, (n, LANES), 1)
    other = jnp.concatenate([-ab[group:], ab[:group]], axis=0)
    mat = jnp.where(lan == sub + n, 1.0, 0.0).astype(F32)
    for k in range(group):
        a = jnp.sum(jnp.where(lan // L == k, ab, 0.0), axis=1, keepdims=True)
        b = jnp.sum(jnp.where(lan // L == k, other, 0.0), axis=1, keepdims=True)
        mat = jnp.where(lan == k, a, mat)
        mat = jnp.where(lan == group + k, b, mat)
    for k in range(n - 1):
        col = jnp.broadcast_to(mat[:, k : k + 1], (n, LANES))
        ratio = col / col[k : k + 1, :]
        mat = mat - jnp.where(sub > k, ratio, 0.0) * mat[k : k + 1, :]
    diag = jnp.sum(jnp.where(lan == sub, mat, 0.0), axis=1, keepdims=True)
    mat = mat / jnp.sqrt(diag)
    cols = [jnp.broadcast_to(mat[:, n + k : n + k + 1], (n, LANES)) for k in range(n)]
    for r in range(n):
        w = [col[r : r + 1, :] for col in cols]
        re = jnp.zeros((quarter, LANES), F32)
        im = jnp.zeros((quarter, LANES), F32)
        for k in range(group):
            re = re + w[k] * img[k, 0] - w[group + k] * img[k, 1]
            im = im + w[k] * img[k, 1] + w[group + k] * img[k, 0]
        out_ref[r, pl.ds(0, quarter, stride=2), :] = re
        out_ref[r, pl.ds(1, quarter, stride=2), :] = im

    for copy in gathers:
        copy.wait_send()
    for d in order:
        sends[d].wait_send()
        swaps[d].wait_send()


def local(n_ka, n_pb, targets, partners, pair_map, shifts):
    L = GRID
    plane = L * L
    bands = targets.shape[1]
    occ = partners.shape[1]
    share = plane // n_pb
    group = LANES // L

    def interleaved(v):
        v = v.reshape(v.shape[0], 2, -1, LANES).transpose(0, 2, 1, 3)
        return v.reshape(v.shape[0], -1, LANES)

    t = interleaved(targets[0])
    p = interleaved(partners[0])
    consts = tables(L, group)
    vmem = pl.BlockSpec(memory_space=pltpu.VMEM)
    smem = pl.BlockSpec(memory_space=pltpu.SMEM)
    dma = pltpu.SemaphoreType.DMA
    out = pl.pallas_call(
        functools.partial(body, n_ka, n_pb),
        out_shape=jax.ShapeDtypeStruct((2 * bands, 2 * share // group, LANES), F32),
        in_specs=[smem, smem] + [vmem] * 6,
        out_specs=vmem,
        scratch_shapes=[
            pltpu.VMEM((n_ka,) + p.shape, BF16),
            pltpu.VMEM(t.shape, F32),
            pltpu.VMEM(p.shape, F32),
            pltpu.VMEM((2, plane, LANES), F32),
            pltpu.VMEM((occ, 2, plane, LANES), F32),
            pltpu.VMEM((2, occ, plane, LANES), BF16),
            pltpu.VMEM((2, plane, LANES), F32),
            pltpu.VMEM((2, plane, LANES), BF16),
            pltpu.VMEM((n_pb - 1, 2, share, LANES), BF16),
            pltpu.VMEM((2 * bands, LANES), F32),
            pltpu.VMEM((n_pb - 1, 2 * bands, LANES), F32),
            pltpu.VMEM((bands, 2, share // group, LANES), F32),
            dma((n_ka - 1,)),
            dma((n_ka - 1,)),
            dma((n_pb - 1,)),
            dma((n_pb - 1,)),
            dma((n_pb - 1,)),
            dma((n_pb - 1,)),
        ],
        compiler_params=pltpu.CompilerParams(collective_id=0, has_side_effects=True),
    )(pair_map, shifts[0], t, p, *consts)
    out = out.reshape(2 * bands, share // group, 2, LANES).transpose(0, 2, 1, 3)
    return out.reshape(1, 2 * bands, 2, share * L)


def solution(mesh):
    return jax.shard_map(
        functools.partial(local, mesh.shape["ka"], mesh.shape["pb"]),
        mesh=mesh,
        in_specs=(
            P("ka", None, None, None),
            P("pb", None, None, "ka"),
            P("ka", "pb"),
            P("ka", "pb", None),
        ),
        out_specs=P("ka", None, None, "pb"),
        check_vma=False,
    )
```

```python
import functools

import jax
import jax.numpy as jnp
import numpy as np
from jax import lax
from jax.experimental import pallas as pl
from jax.experimental.pallas import tpu as pltpu
from jax.sharding import PartitionSpec as P

GRID = 32
KPOINT_SCALING = 2.0
SCREENING_CUTOFF = 0.25
LANES = 128
MESH = pl.DeviceIdType.MESH
F32 = jnp.float32
BF16 = jnp.bfloat16


def tables(length, group):
    n = np.arange(length)
    angle = (n[:, None] * n[None, :] % length) * (2.0 * np.pi / length)
    eye = np.eye(group)
    c = np.kron(eye, np.cos(angle))
    s = np.kron(eye, np.sin(angle))
    fwd = np.block([[c, -s], [s, c]])
    inv = np.block([[c, s], [-s, c]])
    right = np.stack([fwd, inv])
    plain = np.arange(group * length).reshape(group, length)
    turned = plain.reshape(group, length // group, group).transpose(1, 2, 0).ravel()
    mixed = plain.reshape(group, length // group, group).transpose(1, 0, 2).ravel()
    turned = np.concatenate([turned, turned + group * length])
    mixed = np.concatenate([mixed, mixed + group * length])
    left = np.stack([
        fwd.T[turned], fwd.T[mixed][:, mixed], inv.T[mixed][:, mixed], inv.T[:, turned]
    ])
    sel = np.zeros((group, group, length, group, group, length))
    spread = np.zeros((group, length, group, group, length))
    for a in range(group):
        for b in range(group):
            for z in range(length):
                sel[a, b, z, b, a, z] = 1.0
                spread[b, z, b, a, z] = 1.0
    wide = group * group * length
    sel = sel.reshape(wide, wide)
    spread = spread.reshape(group * length, wide)
    return tuple(jnp.asarray(v.astype(BF16)) for v in (right, left, sel, spread))


def dot(a, b):
    return jnp.dot(a, b, preferred_element_type=F32)


def body(
    n_ka, n_pb, pm_ref, sh_ref, p_ref, t_hbm, sel_hbm, spread_hbm, right_hbm, left_hbm, own_ref, mat_ref,
    t_ref, sel_ref, spread_ref, right_ref, left_ref, load_sem, gat, t_de, p_de, t_s, p_s, s, fld, fbf, rcv, ab_snd, ab_rcv,
    g_send, g_recv, f_send, f_recv, a_send, a_recv,
):
    L = GRID
    group = LANES // L
    plane = L * L
    share = plane // n_pb
    block = group * L
    n_blocks = plane // block
    ka = lax.axis_index("ka")
    pb = lax.axis_index("pb")

    barrier = pltpu.get_barrier_semaphore()
    for d in range(1, n_ka):
        pl.semaphore_signal(
            barrier, inc=1, device_id={"ka": lax.rem(ka + d, n_ka), "pb": pb}, device_id_type=MESH
        )
    for d in range(1, n_pb):
        pl.semaphore_signal(
            barrier, inc=1, device_id={"ka": ka, "pb": lax.rem(pb + d, n_pb)}, device_id_type=MESH
        )
    loads = [
        pltpu.make_async_copy(src, dst, load_sem.at[i])
        for i, (src, dst) in enumerate(
            (
                (t_hbm, t_ref),
                (sel_hbm, sel_ref),
                (spread_hbm, spread_ref),
                (right_hbm, right_ref),
                (left_hbm, left_ref),
            )
        )
    ]
    for copy in loads:
        copy.start()
    loads[0].wait()
    t_de[...] = t_ref[...].astype(F32)
    loads[1].wait()
    for c in range(2):
        wide = jnp.concatenate(
            [t_de[i, pl.ds(c, plane // group, stride=2), :].astype(BF16) for i in range(group)], axis=1
        )
        turned = dot(wide, sel_ref[...])
        for y in range(group):
            t_s[c, pl.ds(y, plane // group, stride=group), :] = turned[:, y * LANES : (y + 1) * LANES]

    pl.semaphore_wait(barrier, n_ka + n_pb - 2)
    gathers = []
    for d in range(1, n_ka):
        copy = pltpu.make_async_remote_copy(
            src_ref=p_ref,
            dst_ref=gat.at[ka],
            send_sem=g_send.at[d - 1],
            recv_sem=g_recv.at[d - 1],
            device_id={"ka": lax.rem(ka + d, n_ka), "pb": pb},
            device_id_type=MESH,
        )
        copy.start()
        gathers.append(copy)
    gat[ka] = p_ref[...]

    for copy in loads[2:]:
        copy.wait()

    xs = L // n_ka
    part_rows = xs * L // group

    def spread_part(d):
        for j in range(2):
            p_de[j] = gat[d, j].astype(F32)
            for c in range(2):
                rows = dot(p_de[j, pl.ds(c, part_rows, stride=2), :].astype(BF16), spread_ref[...])
                for y in range(group):
                    p_s[j, c, pl.ds(d * xs * L + y, part_rows, stride=group), :] = rows[
                        :, y * LANES : (y + 1) * LANES
                    ]

    def forward_block(g):
        rows = pl.ds(pl.multiple_of(g * block, block), block)
        tr = t_s[0, rows, :]
        ti = t_s[1, rows, :]
        dens = []
        for j in range(2):
            pr = p_s[j, 0, rows, :]
            pi = p_s[j, 1, rows, :]
            dens.append(
                jnp.concatenate(
                    [(pr * tr + pi * ti).astype(BF16), (pr * ti - pi * tr).astype(BF16)], axis=1
                )
            )
        along_z = dot(jnp.concatenate(dens, axis=0), right_ref[0]).astype(BF16)
        stacked = jnp.concatenate(
            [
                jnp.concatenate([along_z[:block, :LANES], along_z[block:, :LANES]], axis=1),
                jnp.concatenate([along_z[:block, LANES:], along_z[block:, LANES:]], axis=1),
            ],
            axis=0,
        )
        along_y = dot(left_ref[0], stacked)
        for c in range(2):
            for j in range(2):
                s[c, j, rows, :] = along_y[
                    c * block : (c + 1) * block, j * LANES : (j + 1) * LANES
                ].astype(BF16)

    if xs % group == 0:
        per = xs // group
        for d in range(n_ka):
            if d:
                gathers[d - 1].wait_recv()
            owner = lax.rem(ka + n_ka - d, n_ka)
            spread_part(owner)
            for g in range(per):
                forward_block(owner * per + g)
    else:
        for copy in gathers:
            copy.wait_recv()
        for d in range(n_ka):
            spread_part(d)
        lax.fori_loop(0, n_blocks, lambda g, _: (forward_block(g), 0)[1], 0)

    d = pm_ref[0, 0]
    lattice = (d // 16, d // 4 % 4, d % 4)
    offs = [sh_ref[0, a].astype(F32) + lattice[a].astype(F32) * 0.25 for a in range(3)]

    def freq(index, a):
        return (lax.rem(index + L // 2, L) - L // 2).astype(F32) + offs[a]

    row = lax.broadcasted_iota(jnp.int32, (block, LANES), 0)
    lane = lax.broadcasted_iota(jnp.int32, (block, LANES), 1)
    tile = group * group
    fx = freq(row // tile * group + lax.rem(row, group), 0)
    fz = freq(lax.rem(lane, L), 2)
    fxz = fx * fx + fz * fz + SCREENING_CUTOFF
    y_lo = lax.rem(row // group, group)

    for h in range(L // group):
        fy = freq(h * group + y_lo, 1)
        kern = (-KPOINT_SCALING / (L * L * L)) / (fxz + fy * fy)
        stacked = jnp.concatenate(
            [
                jnp.concatenate(
                    [s[c, j, g * block + h * tile : g * block + (h + 1) * tile, :] for j in range(2)], axis=1
                )
                for c in range(2)
                for g in range(n_blocks)
            ],
            axis=0,
        )
        spec = dot(left_ref[1], stacked)
        kk = jnp.concatenate([jnp.concatenate([kern, kern], axis=1)] * 2, axis=0)
        back = dot(left_ref[2], (spec * kk).astype(BF16)).astype(BF16)
        for c in range(2):
            for g in range(n_blocks):
                at = c * block + g * tile
                for j in range(2):
                    s[c, j, g * block + h * tile : g * block + (h + 1) * tile, :] = back[
                        at : at + tile, j * LANES : (j + 1) * LANES
                    ]

    def inverse_block(g):
        rows = pl.ds(pl.multiple_of(g * block, block), block)
        stacked = jnp.concatenate(
            [
                jnp.concatenate([s[c, j, rows, :] for j in range(2)], axis=1)
                for c in range(2)
            ],
            axis=0,
        )
        back_y = dot(left_ref[3], stacked).astype(BF16)
        turned = jnp.concatenate(
            [
                jnp.concatenate(
                    [back_y[:block, j * LANES : (j + 1) * LANES], back_y[block:, j * LANES : (j + 1) * LANES]],
                    axis=1,
                )
                for j in range(2)
            ],
            axis=0,
        )
        pot = dot(turned, right_ref[1])
        fr = jnp.zeros((block, LANES), F32)
        fi = jnp.zeros((block, LANES), F32)
        for j in range(2):
            pr = p_s[j, 0, rows, :]
            pi = p_s[j, 1, rows, :]
            vr = pot[j * block : (j + 1) * block, :LANES]
            vi = pot[j * block : (j + 1) * block, LANES:]
            fr = fr + (pr * vr - pi * vi)
            fi = fi + (pr * vi + pi * vr)
        fld[0, rows, :] = fr
        fld[1, rows, :] = fi
        hr = fr.astype(BF16)
        hi = fi.astype(BF16)
        fbf[0, rows, :] = hr
        fbf[1, rows, :] = hi
        high = jnp.concatenate([hr, hi], axis=1)
        low = jnp.concatenate(
            [(fr - hr.astype(F32)).astype(BF16), (fi - hi.astype(F32)).astype(BF16)], axis=1
        )
        basis = jnp.concatenate([t_s[0, rows, :].astype(BF16), t_s[1, rows, :].astype(BF16)], axis=1)
        dims = (((0,), (0,)), ((), ()))
        return lax.dot_general(basis, high, dims, preferred_element_type=F32) + lax.dot_general(
            basis, low, dims, preferred_element_type=F32
        )

    gram = jnp.zeros((2 * LANES, 2 * LANES), F32)
    order = sorted(range(1, n_pb), key=lambda v: -min(v, n_pb - v))
    split = share % block == 0
    if not split:
        gram = lax.fori_loop(0, n_blocks, lambda g, acc: acc + inverse_block(g), gram)
    sends = {}
    for d in order + [0]:
        to = lax.rem(pb + d, n_pb)
        if split:
            for g in range(share // block):
                gram = gram + inverse_block(to * (share // block) + g)
        if d:
            copy = pltpu.make_async_remote_copy(
                src_ref=fbf.at[:, pl.ds(pl.multiple_of(to * share, share), share), :],
                dst_ref=rcv.at[d - 1],
                send_sem=f_send.at[d - 1],
                recv_sem=f_recv.at[d - 1],
                device_id={"ka": ka, "pb": to},
                device_id_type=MESH,
            )
            if d not in (1, n_pb - 1):
                copy.start()
            sends[d] = copy

    same = gram[:LANES, :LANES] + gram[LANES:, LANES:]
    cross = gram[:LANES, LANES:] - gram[LANES:, :LANES]
    keep = lax.rem(row, L) == lax.rem(lane, L)
    same = jnp.where(keep, same, 0.0)
    cross = jnp.where(keep, cross, 0.0)
    same = same + same.T
    cross = cross - cross.T
    ab = jnp.concatenate(
        [jnp.sum(v[i * L : (i + 1) * L], axis=0, keepdims=True) for v in (same, cross) for i in range(group)],
        axis=0,
    )
    ab_snd[...] = ab
    swaps = {}
    for d in order:
        copy = pltpu.make_async_remote_copy(
            src_ref=ab_snd,
            dst_ref=ab_rcv.at[d - 1],
            send_sem=a_send.at[d - 1],
            recv_sem=a_recv.at[d - 1],
            device_id={"ka": ka, "pb": lax.rem(pb + d, n_pb)},
            device_id_type=MESH,
        )
        copy.start()
        swaps[d] = copy

    for d in order:
        if d in (1, n_pb - 1):
            sends[d].start()

    for d in order:
        swaps[d].wait_recv()
        ab = ab + ab_rcv[d - 1]
    ab = ab * (-0.5 / (L * L * L))
    n = 2 * group
    sub = lax.broadcasted_iota(jnp.int32, (n, LANES), 0)
    lan = lax.broadcasted_iota(jnp.int32, (n, LANES), 1)
    other = jnp.concatenate([-ab[group:], ab[:group]], axis=0)
    mat = jnp.where(lan == sub + n, 1.0, 0.0).astype(F32)
    for k in range(group):
        a = jnp.sum(jnp.where(lan // L == k, ab, 0.0), axis=1, keepdims=True)
        b = jnp.sum(jnp.where(lan // L == k, other, 0.0), axis=1, keepdims=True)
        mat = jnp.where(lan == k, a, mat)
        mat = jnp.where(lan == group + k, b, mat)
    for k in range(n - 1):
        col = jnp.broadcast_to(mat[:, k : k + 1], (n, LANES))
        ratio = col / col[k : k + 1, :]
        mat = mat - jnp.where(sub > k, ratio, 0.0) * mat[k : k + 1, :]
    diag = jnp.sum(jnp.where(lan == sub, mat, 0.0), axis=1, keepdims=True)
    mat = mat / jnp.sqrt(diag)
    mat_ref[...] = mat

    own = pl.multiple_of(pb * share, share)
    for d in order:
        sends[d].wait_recv()
    for c in range(2):
        total = fld[c, pl.ds(own, share), :]
        for d in order:
            total = total + rcv[d - 1, c].astype(F32)
        own_ref[c] = total

    for copy in gathers:
        copy.wait_send()
    for d in order:
        sends[d].wait_send()
        swaps[d].wait_send()


def project(mat_ref, own_ref, out_ref):
    L = GRID
    group = LANES // L
    n = 2 * group
    mat = mat_ref[...]
    img = {}
    quarter = own_ref.shape[1] // group
    lane_q = lax.broadcasted_iota(jnp.int32, (quarter, LANES), 1) // L
    for c in range(2):
        rows = [own_ref[c, pl.ds(y, quarter, stride=group), :] for y in range(group)]
        for k in range(group):
            turned = jnp.zeros((quarter, LANES), F32)
            for y in range(group):
                shift = (y - k) % group * L
                moved = pltpu.roll(rows[y], shift, 1) if shift else rows[y]
                turned = jnp.where(lane_q == y, moved, turned)
            img[k, c] = turned

    cols = [jnp.broadcast_to(mat[:, n + k : n + k + 1], (n, LANES)) for k in range(n)]
    for r in range(n):
        w = [col[r : r + 1, :] for col in cols]
        re = jnp.zeros((quarter, LANES), F32)
        im = jnp.zeros((quarter, LANES), F32)
        for k in range(group):
            re = re + w[k] * img[k, 0] - w[group + k] * img[k, 1]
            im = im + w[k] * img[k, 1] + w[group + k] * img[k, 0]
        out_ref[r, pl.ds(0, quarter, stride=2), :] = re
        out_ref[r, pl.ds(1, quarter, stride=2), :] = im


def local(n_ka, n_pb, targets, partners, pair_map, shifts):
    L = GRID
    plane = L * L
    bands = targets.shape[1]
    occ = partners.shape[1]
    share = plane // n_pb
    group = LANES // L

    def interleaved(v):
        v = v.reshape(v.shape[0], 2, -1, LANES).transpose(0, 2, 1, 3)
        return v.reshape(v.shape[0], -1, LANES)

    t = interleaved(targets[0])
    p = interleaved(partners[0])
    consts = tables(L, group)
    vmem = pl.BlockSpec(memory_space=pltpu.VMEM)
    smem = pl.BlockSpec(memory_space=pltpu.SMEM)
    dma = pltpu.SemaphoreType.DMA
    hbm = pl.BlockSpec(memory_space=pltpu.HBM)
    right, left, sel, spread = consts
    own, mat = pl.pallas_call(
        functools.partial(body, n_ka, n_pb),
        out_shape=(
            jax.ShapeDtypeStruct((2, share, LANES), F32),
            jax.ShapeDtypeStruct((2 * bands, LANES), F32),
        ),
        in_specs=[smem, smem, vmem] + [hbm] * 5,
        out_specs=(vmem, vmem),
        scratch_shapes=[
            pltpu.VMEM(t.shape, BF16),
            pltpu.VMEM(sel.shape, BF16),
            pltpu.VMEM(spread.shape, BF16),
            pltpu.VMEM(right.shape, BF16),
            pltpu.VMEM(left.shape, BF16),
            dma((5,)),
            pltpu.VMEM((n_ka,) + p.shape, BF16),
            pltpu.VMEM(t.shape, F32),
            pltpu.VMEM(p.shape, F32),
            pltpu.VMEM((2, plane, LANES), F32),
            pltpu.VMEM((occ, 2, plane, LANES), F32),
            pltpu.VMEM((2, occ, plane, LANES), BF16),
            pltpu.VMEM((2, plane, LANES), F32),
            pltpu.VMEM((2, plane, LANES), BF16),
            pltpu.VMEM((n_pb - 1, 2, share, LANES), BF16),
            pltpu.VMEM((2 * bands, LANES), F32),
            pltpu.VMEM((n_pb - 1, 2 * bands, LANES), F32),
            dma((n_ka - 1,)),
            dma((n_ka - 1,)),
            dma((n_pb - 1,)),
            dma((n_pb - 1,)),
            dma((n_pb - 1,)),
            dma((n_pb - 1,)),
        ],
        compiler_params=pltpu.CompilerParams(collective_id=0, has_side_effects=True),
    )(pair_map, shifts[0], p, t, sel, spread, right, left)
    steps = 2
    out = pl.pallas_call(
        project,
        grid=(steps,),
        out_shape=jax.ShapeDtypeStruct((2 * bands, 2 * share // group, LANES), F32),
        in_specs=[
            pl.BlockSpec((2 * bands, LANES), lambda i: (0, 0)),
            pl.BlockSpec((2, share // steps, LANES), lambda i: (0, i, 0)),
        ],
        out_specs=pl.BlockSpec((2 * bands, 2 * share // group // steps, LANES), lambda i: (0, i, 0)),
    )(mat, own)
    out = out.reshape(2 * bands, share // group, 2, LANES).transpose(0, 2, 1, 3)
    return out.reshape(1, 2 * bands, 2, share * L)


def solution(mesh):
    return jax.shard_map(
        functools.partial(local, mesh.shape["ka"], mesh.shape["pb"]),
        mesh=mesh,
        in_specs=(
            P("ka", None, None, None),
            P("pb", None, None, "ka"),
            P("ka", "pb"),
            P("ka", "pb", None),
        ),
        out_specs=P("ka", None, None, "pb"),
        check_vma=False,
    )
```

```python
import functools

import jax
import jax.numpy as jnp
import numpy as np
from jax import lax
from jax.experimental import pallas as pl
from jax.experimental.pallas import tpu as pltpu
from jax.sharding import PartitionSpec as P

GRID = 32
KPOINT_SCALING = 2.0
SCREENING_CUTOFF = 0.25
LANES = 128
MESH = pl.DeviceIdType.MESH
F32 = jnp.float32
BF16 = jnp.bfloat16


def tables(length, group):
    n = np.arange(length)
    angle = (n[:, None] * n[None, :] % length) * (2.0 * np.pi / length)
    eye = np.eye(group)
    c = np.kron(eye, np.cos(angle))
    s = np.kron(eye, np.sin(angle))
    fwd = np.block([[c, -s], [s, c]])
    inv = np.block([[c, s], [-s, c]])
    right = np.stack([fwd, inv])
    plain = np.arange(group * length).reshape(group, length)
    turned = plain.reshape(group, length // group, group).transpose(1, 2, 0).ravel()
    mixed = plain.reshape(group, length // group, group).transpose(1, 0, 2).ravel()
    turned = np.concatenate([turned, turned + group * length])
    mixed = np.concatenate([mixed, mixed + group * length])
    left = np.stack([
        fwd.T[turned], fwd.T[mixed][:, mixed], inv.T[mixed][:, mixed], inv.T[:, turned]
    ])
    sel = np.zeros((group, group, length, group, group, length))
    spread = np.zeros((group, length, group, group, length))
    for a in range(group):
        for b in range(group):
            for z in range(length):
                sel[a, b, z, b, a, z] = 1.0
                spread[b, z, b, a, z] = 1.0
    wide = group * group * length
    sel = sel.reshape(wide, wide)
    spread = spread.reshape(group * length, wide)
    return tuple(jnp.asarray(v.astype(BF16)) for v in (right, left, sel, spread))


def dot(a, b):
    return jnp.dot(a, b, preferred_element_type=F32)


def body(
    n_ka, n_pb, pm_ref, sh_ref, p_ref, t_hbm, sel_hbm, spread_hbm, right_hbm, left_hbm, own_ref, mat_ref,
    t_ref, sel_ref, spread_ref, right_ref, left_ref, load_sem, gat, t_de, p_de, t_s, p_s, s, fld, fbf, rcv, ab_snd, ab_rcv,
    g_send, g_recv, f_send, f_recv, a_send, a_recv,
):
    L = GRID
    group = LANES // L
    plane = L * L
    share = plane // n_pb
    block = group * L
    n_blocks = plane // block
    ka = lax.axis_index("ka")
    pb = lax.axis_index("pb")

    barrier = pltpu.get_barrier_semaphore()
    for d in range(1, n_ka):
        pl.semaphore_signal(
            barrier, inc=1, device_id={"ka": lax.rem(ka + d, n_ka), "pb": pb}, device_id_type=MESH
        )
    for d in range(1, n_pb):
        pl.semaphore_signal(
            barrier, inc=1, device_id={"ka": ka, "pb": lax.rem(pb + d, n_pb)}, device_id_type=MESH
        )
    loads = [
        pltpu.make_async_copy(src, dst, load_sem.at[i])
        for i, (src, dst) in enumerate(
            (
                (t_hbm, t_ref),
                (sel_hbm, sel_ref),
                (spread_hbm, spread_ref),
                (right_hbm, right_ref),
                (left_hbm, left_ref),
            )
        )
    ]
    for copy in loads:
        copy.start()
    loads[0].wait()
    t_de[...] = t_ref[...].astype(F32)
    loads[1].wait()
    for c in range(2):
        wide = jnp.concatenate(
            [t_de[i, pl.ds(c, plane // group, stride=2), :].astype(BF16) for i in range(group)], axis=1
        )
        turned = dot(wide, sel_ref[...])
        for y in range(group):
            t_s[c, pl.ds(y, plane // group, stride=group), :] = turned[:, y * LANES : (y + 1) * LANES]

    pl.semaphore_wait(barrier, n_ka + n_pb - 2)
    gathers = []
    for d in range(1, n_ka):
        copy = pltpu.make_async_remote_copy(
            src_ref=p_ref,
            dst_ref=gat.at[ka],
            send_sem=g_send.at[d - 1],
            recv_sem=g_recv.at[d - 1],
            device_id={"ka": lax.rem(ka + d, n_ka), "pb": pb},
            device_id_type=MESH,
        )
        copy.start()
        gathers.append(copy)
    gat[ka] = p_ref[...]

    for copy in loads[2:]:
        copy.wait()

    xs = L // n_ka
    part_rows = xs * L // group

    def spread_part(d):
        for j in range(2):
            p_de[j] = gat[d, j].astype(F32)
            for c in range(2):
                rows = dot(p_de[j, pl.ds(c, part_rows, stride=2), :].astype(BF16), spread_ref[...])
                for y in range(group):
                    p_s[j, c, pl.ds(d * xs * L + y, part_rows, stride=group), :] = rows[
                        :, y * LANES : (y + 1) * LANES
                    ]

    def forward_block(g):
        rows = pl.ds(pl.multiple_of(g * block, block), block)
        tr = t_s[0, rows, :]
        ti = t_s[1, rows, :]
        dens = []
        for j in range(2):
            pr = p_s[j, 0, rows, :]
            pi = p_s[j, 1, rows, :]
            dens.append(
                jnp.concatenate(
                    [(pr * tr + pi * ti).astype(BF16), (pr * ti - pi * tr).astype(BF16)], axis=1
                )
            )
        along_z = dot(jnp.concatenate(dens, axis=0), right_ref[0]).astype(BF16)
        stacked = jnp.concatenate(
            [
                jnp.concatenate([along_z[:block, :LANES], along_z[block:, :LANES]], axis=1),
                jnp.concatenate([along_z[:block, LANES:], along_z[block:, LANES:]], axis=1),
            ],
            axis=0,
        )
        along_y = dot(left_ref[0], stacked)
        for c in range(2):
            for j in range(2):
                s[c, j, rows, :] = along_y[
                    c * block : (c + 1) * block, j * LANES : (j + 1) * LANES
                ].astype(BF16)

    if xs % group == 0:
        per = xs // group
        for d in range(n_ka):
            if d:
                gathers[d - 1].wait_recv()
            owner = lax.rem(ka + n_ka - d, n_ka)
            spread_part(owner)
            for g in range(per):
                forward_block(owner * per + g)
    else:
        for copy in gathers:
            copy.wait_recv()
        for d in range(n_ka):
            spread_part(d)
        lax.fori_loop(0, n_blocks, lambda g, _: (forward_block(g), 0)[1], 0)

    d = pm_ref[0, 0]
    lattice = (d // 16, d // 4 % 4, d % 4)
    offs = [sh_ref[0, a].astype(F32) + lattice[a].astype(F32) * 0.25 for a in range(3)]

    def freq(index, a):
        return (lax.rem(index + L // 2, L) - L // 2).astype(F32) + offs[a]

    row = lax.broadcasted_iota(jnp.int32, (block, LANES), 0)
    lane = lax.broadcasted_iota(jnp.int32, (block, LANES), 1)
    tile = group * group
    fx = freq(row // tile * group + lax.rem(row, group), 0)
    fz = freq(lax.rem(lane, L), 2)
    fxz = fx * fx + fz * fz + SCREENING_CUTOFF
    y_lo = lax.rem(row // group, group)

    for h in range(L // group):
        fy = freq(h * group + y_lo, 1)
        kern = (-KPOINT_SCALING / (L * L * L)) / (fxz + fy * fy)
        stacked = jnp.concatenate(
            [
                jnp.concatenate(
                    [s[c, j, g * block + h * tile : g * block + (h + 1) * tile, :] for j in range(2)], axis=1
                )
                for c in range(2)
                for g in range(n_blocks)
            ],
            axis=0,
        )
        spec = dot(left_ref[1], stacked)
        kk = jnp.concatenate([jnp.concatenate([kern, kern], axis=1)] * 2, axis=0)
        back = dot(left_ref[2], (spec * kk).astype(BF16)).astype(BF16)
        for c in range(2):
            for g in range(n_blocks):
                at = c * block + g * tile
                for j in range(2):
                    s[c, j, g * block + h * tile : g * block + (h + 1) * tile, :] = back[
                        at : at + tile, j * LANES : (j + 1) * LANES
                    ]

    def inverse_block(g):
        rows = pl.ds(pl.multiple_of(g * block, block), block)
        stacked = jnp.concatenate(
            [
                jnp.concatenate([s[c, j, rows, :] for j in range(2)], axis=1)
                for c in range(2)
            ],
            axis=0,
        )
        back_y = dot(left_ref[3], stacked).astype(BF16)
        turned = jnp.concatenate(
            [
                jnp.concatenate(
                    [back_y[:block, j * LANES : (j + 1) * LANES], back_y[block:, j * LANES : (j + 1) * LANES]],
                    axis=1,
                )
                for j in range(2)
            ],
            axis=0,
        )
        pot = dot(turned, right_ref[1])
        fr = jnp.zeros((block, LANES), F32)
        fi = jnp.zeros((block, LANES), F32)
        for j in range(2):
            pr = p_s[j, 0, rows, :]
            pi = p_s[j, 1, rows, :]
            vr = pot[j * block : (j + 1) * block, :LANES]
            vi = pot[j * block : (j + 1) * block, LANES:]
            fr = fr + (pr * vr - pi * vi)
            fi = fi + (pr * vi + pi * vr)
        fld[0, rows, :] = fr
        fld[1, rows, :] = fi
        hr = fr.astype(BF16)
        hi = fi.astype(BF16)
        fbf[0, rows, :] = hr
        fbf[1, rows, :] = hi
        high = jnp.concatenate([hr, hi], axis=1)
        low = jnp.concatenate(
            [(fr - hr.astype(F32)).astype(BF16), (fi - hi.astype(F32)).astype(BF16)], axis=1
        )
        basis = jnp.concatenate([t_s[0, rows, :].astype(BF16), t_s[1, rows, :].astype(BF16)], axis=1)
        dims = (((0,), (0,)), ((), ()))
        return lax.dot_general(basis, high, dims, preferred_element_type=F32) + lax.dot_general(
            basis, low, dims, preferred_element_type=F32
        )

    gram = jnp.zeros((2 * LANES, 2 * LANES), F32)
    order = sorted(range(1, n_pb), key=lambda v: -min(v, n_pb - v))
    split = share % block == 0
    if not split:
        gram = lax.fori_loop(0, n_blocks, lambda g, acc: acc + inverse_block(g), gram)
    sends = {}
    ring = n_pb == 4

    def rows_of(d):
        return pl.ds(pl.multiple_of(lax.rem(pb + d, n_pb) * share, share), share)

    def ring_copy(slot, to, source, target):
        return pltpu.make_async_remote_copy(
            src_ref=source,
            dst_ref=target,
            send_sem=f_send.at[slot],
            recv_sem=f_recv.at[slot],
            device_id={"ka": ka, "pb": lax.rem(pb + to, n_pb)},
            device_id_type=MESH,
        )

    if ring:
        sides = (1, n_pb - 1)
        relays = [ring_copy(c, sides[c], fbf.at[c, rows_of(2)], rcv.at[2, c]) for c in range(2)]
        early = [ring_copy(2 + i, sides[i], fbf.at[1 - i, rows_of(sides[i])], rcv.at[i, 1 - i]) for i in range(2)]
        late = [ring_copy(4 + i, sides[i], fbf.at[i, rows_of(sides[i])], rcv.at[i, i]) for i in range(2)]
    for d in order + [0]:
        to = lax.rem(pb + d, n_pb)
        if split:
            for g in range(share // block):
                gram = gram + inverse_block(to * (share // block) + g)
        if ring and d == 2:
            for copy in relays:
                copy.start()
        if d and not ring:
            copy = pltpu.make_async_remote_copy(
                src_ref=fbf.at[:, pl.ds(pl.multiple_of(to * share, share), share), :],
                dst_ref=rcv.at[d - 1],
                send_sem=f_send.at[d - 1],
                recv_sem=f_recv.at[d - 1],
                device_id={"ka": ka, "pb": to},
                device_id_type=MESH,
            )
            if d not in (1, n_pb - 1):
                copy.start()
            sends[d] = copy

    same = gram[:LANES, :LANES] + gram[LANES:, LANES:]
    cross = gram[:LANES, LANES:] - gram[LANES:, :LANES]
    keep = lax.rem(row, L) == lax.rem(lane, L)
    same = jnp.where(keep, same, 0.0)
    cross = jnp.where(keep, cross, 0.0)
    same = same + same.T
    cross = cross - cross.T
    ab = jnp.concatenate(
        [jnp.sum(v[i * L : (i + 1) * L], axis=0, keepdims=True) for v in (same, cross) for i in range(group)],
        axis=0,
    )
    ab_snd[...] = ab
    swaps = {}
    for d in order:
        copy = pltpu.make_async_remote_copy(
            src_ref=ab_snd,
            dst_ref=ab_rcv.at[d - 1],
            send_sem=a_send.at[d - 1],
            recv_sem=a_recv.at[d - 1],
            device_id={"ka": ka, "pb": lax.rem(pb + d, n_pb)},
            device_id_type=MESH,
        )
        copy.start()
        swaps[d] = copy

    if ring:
        for copy in early:
            copy.start()
        for i in range(2):
            relays[i].wait_recv()
            rows = rows_of(sides[i])
            fbf[i, rows, :] = (fld[i, rows, :] + rcv[2, i].astype(F32)).astype(BF16)
            late[i].start()
    for d in order:
        if not ring and d in (1, n_pb - 1):
            sends[d].start()

    for d in order:
        swaps[d].wait_recv()
        ab = ab + ab_rcv[d - 1]
    ab = ab * (-0.5 / (L * L * L))
    n = 2 * group
    sub = lax.broadcasted_iota(jnp.int32, (n, LANES), 0)
    lan = lax.broadcasted_iota(jnp.int32, (n, LANES), 1)
    other = jnp.concatenate([-ab[group:], ab[:group]], axis=0)
    mat = jnp.where(lan == sub + n, 1.0, 0.0).astype(F32)
    for k in range(group):
        a = jnp.sum(jnp.where(lan // L == k, ab, 0.0), axis=1, keepdims=True)
        b = jnp.sum(jnp.where(lan // L == k, other, 0.0), axis=1, keepdims=True)
        mat = jnp.where(lan == k, a, mat)
        mat = jnp.where(lan == group + k, b, mat)
    for k in range(n - 1):
        col = jnp.broadcast_to(mat[:, k : k + 1], (n, LANES))
        ratio = col / col[k : k + 1, :]
        mat = mat - jnp.where(sub > k, ratio, 0.0) * mat[k : k + 1, :]
    diag = jnp.sum(jnp.where(lan == sub, mat, 0.0), axis=1, keepdims=True)
    mat = mat / jnp.sqrt(diag)
    mat_ref[...] = mat

    own = pl.multiple_of(pb * share, share)
    for copy in early + late if ring else [sends[d] for d in order]:
        copy.wait_recv()
    for c in range(2):
        total = fld[c, pl.ds(own, share), :]
        for slot in range(2 if ring else n_pb - 1):
            total = total + rcv[slot, c].astype(F32)
        own_ref[c] = total

    for copy in gathers:
        copy.wait_send()
    for copy in relays + early + late if ring else [sends[d] for d in order]:
        copy.wait_send()
    for d in order:
        swaps[d].wait_send()


def project(mat_ref, own_ref, out_ref):
    L = GRID
    group = LANES // L
    n = 2 * group
    mat = mat_ref[...]
    img = {}
    quarter = own_ref.shape[1] // group
    lane_q = lax.broadcasted_iota(jnp.int32, (quarter, LANES), 1) // L
    for c in range(2):
        rows = [own_ref[c, pl.ds(y, quarter, stride=group), :] for y in range(group)]
        for k in range(group):
            turned = jnp.zeros((quarter, LANES), F32)
            for y in range(group):
                shift = (y - k) % group * L
                moved = pltpu.roll(rows[y], shift, 1) if shift else rows[y]
                turned = jnp.where(lane_q == y, moved, turned)
            img[k, c] = turned

    cols = [jnp.broadcast_to(mat[:, n + k : n + k + 1], (n, LANES)) for k in range(n)]
    for r in range(n):
        w = [col[r : r + 1, :] for col in cols]
        re = jnp.zeros((quarter, LANES), F32)
        im = jnp.zeros((quarter, LANES), F32)
        for k in range(group):
            re = re + w[k] * img[k, 0] - w[group + k] * img[k, 1]
            im = im + w[k] * img[k, 1] + w[group + k] * img[k, 0]
        out_ref[r, pl.ds(0, quarter, stride=2), :] = re
        out_ref[r, pl.ds(1, quarter, stride=2), :] = im


def local(n_ka, n_pb, targets, partners, pair_map, shifts):
    L = GRID
    plane = L * L
    bands = targets.shape[1]
    occ = partners.shape[1]
    share = plane // n_pb
    group = LANES // L

    def interleaved(v):
        v = v.reshape(v.shape[0], 2, -1, LANES).transpose(0, 2, 1, 3)
        return v.reshape(v.shape[0], -1, LANES)

    t = interleaved(targets[0])
    p = interleaved(partners[0])
    consts = tables(L, group)
    vmem = pl.BlockSpec(memory_space=pltpu.VMEM)
    smem = pl.BlockSpec(memory_space=pltpu.SMEM)
    dma = pltpu.SemaphoreType.DMA
    hbm = pl.BlockSpec(memory_space=pltpu.HBM)
    right, left, sel, spread = consts
    own, mat = pl.pallas_call(
        functools.partial(body, n_ka, n_pb),
        out_shape=(
            jax.ShapeDtypeStruct((2, share, LANES), F32),
            jax.ShapeDtypeStruct((2 * bands, LANES), F32),
        ),
        in_specs=[smem, smem, vmem] + [hbm] * 5,
        out_specs=(vmem, vmem),
        scratch_shapes=[
            pltpu.VMEM(t.shape, BF16),
            pltpu.VMEM(sel.shape, BF16),
            pltpu.VMEM(spread.shape, BF16),
            pltpu.VMEM(right.shape, BF16),
            pltpu.VMEM(left.shape, BF16),
            dma((5,)),
            pltpu.VMEM((n_ka,) + p.shape, BF16),
            pltpu.VMEM(t.shape, F32),
            pltpu.VMEM(p.shape, F32),
            pltpu.VMEM((2, plane, LANES), F32),
            pltpu.VMEM((occ, 2, plane, LANES), F32),
            pltpu.VMEM((2, occ, plane, LANES), BF16),
            pltpu.VMEM((2, plane, LANES), F32),
            pltpu.VMEM((2, plane, LANES), BF16),
            pltpu.VMEM((n_pb - 1, 2, share, LANES), BF16),
            pltpu.VMEM((2 * bands, LANES), F32),
            pltpu.VMEM((n_pb - 1, 2 * bands, LANES), F32),
            dma((n_ka - 1,)),
            dma((n_ka - 1,)),
            dma((2 * n_pb,)),
            dma((2 * n_pb,)),
            dma((n_pb - 1,)),
            dma((n_pb - 1,)),
        ],
        compiler_params=pltpu.CompilerParams(collective_id=0, has_side_effects=True),
    )(pair_map, shifts[0], p, t, sel, spread, right, left)
    steps = 2
    out = pl.pallas_call(
        project,
        grid=(steps,),
        out_shape=jax.ShapeDtypeStruct((2 * bands, 2 * share // group, LANES), F32),
        in_specs=[
            pl.BlockSpec((2 * bands, LANES), lambda i: (0, 0)),
            pl.BlockSpec((2, share // steps, LANES), lambda i: (0, i, 0)),
        ],
        out_specs=pl.BlockSpec((2 * bands, 2 * share // group // steps, LANES), lambda i: (0, i, 0)),
    )(mat, own)
    out = out.reshape(2 * bands, share // group, 2, LANES).transpose(0, 2, 1, 3)
    return out.reshape(1, 2 * bands, 2, share * L)


def solution(mesh):
    return jax.shard_map(
        functools.partial(local, mesh.shape["ka"], mesh.shape["pb"]),
        mesh=mesh,
        in_specs=(
            P("ka", None, None, None),
            P("pb", None, None, "ka"),
            P("ka", "pb"),
            P("ka", "pb", None),
        ),
        out_specs=P("ka", None, None, "pb"),
        check_vma=False,
    )
```

```python
import functools

import jax
import jax.numpy as jnp
import numpy as np
from jax import lax
from jax.experimental import pallas as pl
from jax.experimental.pallas import tpu as pltpu
from jax.sharding import PartitionSpec as P

GRID = 32
KPOINT_SCALING = 2.0
SCREENING_CUTOFF = 0.25
LANES = 128
MESH = pl.DeviceIdType.MESH
F32 = jnp.float32
BF16 = jnp.bfloat16


def tables(length, group):
    n = np.arange(length)
    angle = (n[:, None] * n[None, :] % length) * (2.0 * np.pi / length)
    eye = np.eye(group)
    c = np.kron(eye, np.cos(angle))
    s = np.kron(eye, np.sin(angle))
    fwd = np.block([[c, -s], [s, c]])
    inv = np.block([[c, s], [-s, c]])
    right = np.stack([fwd, inv])
    plain = np.arange(group * length).reshape(group, length)
    turned = plain.reshape(group, length // group, group).transpose(1, 2, 0).ravel()
    mixed = plain.reshape(group, length // group, group).transpose(1, 0, 2).ravel()
    turned = np.concatenate([turned, turned + group * length])
    mixed = np.concatenate([mixed, mixed + group * length])
    left = np.stack([
        fwd.T[turned], fwd.T[mixed][:, mixed], inv.T[mixed][:, mixed], inv.T[:, turned]
    ])
    sel = np.zeros((group, group, length, group, group, length))
    spread = np.zeros((group, length, group, group, length))
    for a in range(group):
        for b in range(group):
            for z in range(length):
                sel[a, b, z, b, a, z] = 1.0
                spread[b, z, b, a, z] = 1.0
    wide = group * group * length
    sel = sel.reshape(wide, wide)
    spread = spread.reshape(group * length, wide)
    return tuple(jnp.asarray(v.astype(BF16)) for v in (right, left, sel, spread))


def dot(a, b):
    return jnp.dot(a, b, preferred_element_type=F32)


def body(
    n_ka, n_pb, pm_ref, sh_ref, p_ref, t_hbm, sel_hbm, spread_hbm, right_hbm, left_hbm, own_ref, mat_ref,
    t_ref, sel_ref, spread_ref, right_ref, left_ref, load_sem, gat, t_de, p_de, t_s, p_s, s, fld, fbf, rcv, ab_snd, ab_rcv,
    g_send, g_recv, f_send, f_recv, a_send, a_recv,
):
    L = GRID
    group = LANES // L
    plane = L * L
    share = plane // n_pb
    block = group * L
    n_blocks = plane // block
    ka = lax.axis_index("ka")
    pb = lax.axis_index("pb")

    barrier = pltpu.get_barrier_semaphore()
    for d in range(1, n_ka):
        pl.semaphore_signal(
            barrier, inc=1, device_id={"ka": lax.rem(ka + d, n_ka), "pb": pb}, device_id_type=MESH
        )
    for d in range(1, n_pb):
        pl.semaphore_signal(
            barrier, inc=1, device_id={"ka": ka, "pb": lax.rem(pb + d, n_pb)}, device_id_type=MESH
        )
    loads = [
        pltpu.make_async_copy(src, dst, load_sem.at[i])
        for i, (src, dst) in enumerate(
            (
                (t_hbm, t_ref),
                (sel_hbm, sel_ref),
                (spread_hbm, spread_ref),
                (right_hbm, right_ref),
                (left_hbm, left_ref),
            )
        )
    ]
    for copy in loads:
        copy.start()
    loads[0].wait()
    t_de[...] = t_ref[...].astype(F32)
    loads[1].wait()
    for c in range(2):
        wide = jnp.concatenate(
            [t_de[i, pl.ds(c, plane // group, stride=2), :].astype(BF16) for i in range(group)], axis=1
        )
        turned = dot(wide, sel_ref[...])
        for y in range(group):
            t_s[c, pl.ds(y, plane // group, stride=group), :] = turned[:, y * LANES : (y + 1) * LANES]

    pl.semaphore_wait(barrier, n_ka + n_pb - 2)
    gathers = []
    for d in range(1, n_ka):
        copy = pltpu.make_async_remote_copy(
            src_ref=p_ref,
            dst_ref=gat.at[ka],
            send_sem=g_send.at[d - 1],
            recv_sem=g_recv.at[d - 1],
            device_id={"ka": lax.rem(ka + d, n_ka), "pb": pb},
            device_id_type=MESH,
        )
        copy.start()
        gathers.append(copy)
    gat[ka] = p_ref[...]

    for copy in loads[2:]:
        copy.wait()

    xs = L // n_ka
    part_rows = xs * L // group

    def spread_part(d):
        for j in range(2):
            p_de[j] = gat[d, j].astype(F32)
            for c in range(2):
                rows = dot(p_de[j, pl.ds(c, part_rows, stride=2), :].astype(BF16), spread_ref[...])
                for y in range(group):
                    p_s[j, c, pl.ds(d * xs * L + y, part_rows, stride=group), :] = rows[
                        :, y * LANES : (y + 1) * LANES
                    ]

    def forward_block(g):
        rows = pl.ds(pl.multiple_of(g * block, block), block)
        tr = t_s[0, rows, :]
        ti = t_s[1, rows, :]
        dens = []
        for j in range(2):
            pr = p_s[j, 0, rows, :]
            pi = p_s[j, 1, rows, :]
            dens.append(
                jnp.concatenate(
                    [(pr * tr + pi * ti).astype(BF16), (pr * ti - pi * tr).astype(BF16)], axis=1
                )
            )
        along_z = dot(jnp.concatenate(dens, axis=0), right_ref[0]).astype(BF16)
        stacked = jnp.concatenate(
            [
                jnp.concatenate([along_z[:block, :LANES], along_z[block:, :LANES]], axis=1),
                jnp.concatenate([along_z[:block, LANES:], along_z[block:, LANES:]], axis=1),
            ],
            axis=0,
        )
        along_y = dot(left_ref[0], stacked)
        for c in range(2):
            for j in range(2):
                s[c, j, rows, :] = along_y[
                    c * block : (c + 1) * block, j * LANES : (j + 1) * LANES
                ].astype(BF16)

    if xs % group == 0:
        per = xs // group
        for d in range(n_ka):
            if d:
                gathers[d - 1].wait_recv()
            owner = lax.rem(ka + n_ka - d, n_ka)
            spread_part(owner)
            for g in range(per):
                forward_block(owner * per + g)
    else:
        for copy in gathers:
            copy.wait_recv()
        for d in range(n_ka):
            spread_part(d)
        lax.fori_loop(0, n_blocks, lambda g, _: (forward_block(g), 0)[1], 0)

    d = pm_ref[0, 0]
    lattice = (d // 16, d // 4 % 4, d % 4)
    offs = [sh_ref[0, a].astype(F32) + lattice[a].astype(F32) * 0.25 for a in range(3)]

    def freq(index, a):
        return (lax.rem(index + L // 2, L) - L // 2).astype(F32) + offs[a]

    row = lax.broadcasted_iota(jnp.int32, (block, LANES), 0)
    lane = lax.broadcasted_iota(jnp.int32, (block, LANES), 1)
    tile = group * group
    fx = freq(row // tile * group + lax.rem(row, group), 0)
    fz = freq(lax.rem(lane, L), 2)
    fxz = fx * fx + fz * fz + SCREENING_CUTOFF
    y_lo = lax.rem(row // group, group)

    for h in range(L // group):
        fy = freq(h * group + y_lo, 1)
        kern = (-KPOINT_SCALING / (L * L * L)) / (fxz + fy * fy)
        stacked = jnp.concatenate(
            [
                jnp.concatenate(
                    [s[c, j, g * block + h * tile : g * block + (h + 1) * tile, :] for j in range(2)], axis=1
                )
                for c in range(2)
                for g in range(n_blocks)
            ],
            axis=0,
        )
        spec = dot(left_ref[1], stacked)
        kk = jnp.concatenate([jnp.concatenate([kern, kern], axis=1)] * 2, axis=0)
        back = dot(left_ref[2], (spec * kk).astype(BF16)).astype(BF16)
        for c in range(2):
            for g in range(n_blocks):
                at = c * block + g * tile
                for j in range(2):
                    s[c, j, g * block + h * tile : g * block + (h + 1) * tile, :] = back[
                        at : at + tile, j * LANES : (j + 1) * LANES
                    ]

    def inverse_block(g):
        rows = pl.ds(pl.multiple_of(g * block, block), block)
        stacked = jnp.concatenate(
            [
                jnp.concatenate([s[c, j, rows, :] for j in range(2)], axis=1)
                for c in range(2)
            ],
            axis=0,
        )
        back_y = dot(left_ref[3], stacked).astype(BF16)
        turned = jnp.concatenate(
            [
                jnp.concatenate(
                    [back_y[:block, j * LANES : (j + 1) * LANES], back_y[block:, j * LANES : (j + 1) * LANES]],
                    axis=1,
                )
                for j in range(2)
            ],
            axis=0,
        )
        pot = dot(turned, right_ref[1])
        fr = jnp.zeros((block, LANES), F32)
        fi = jnp.zeros((block, LANES), F32)
        for j in range(2):
            pr = p_s[j, 0, rows, :]
            pi = p_s[j, 1, rows, :]
            vr = pot[j * block : (j + 1) * block, :LANES]
            vi = pot[j * block : (j + 1) * block, LANES:]
            fr = fr + (pr * vr - pi * vi)
            fi = fi + (pr * vi + pi * vr)
        fld[0, rows, :] = fr
        fld[1, rows, :] = fi
        hr = fr.astype(BF16)
        hi = fi.astype(BF16)
        fbf[0, rows, :] = hr
        fbf[1, rows, :] = hi
        high = jnp.concatenate([hr, hi], axis=1)
        low = jnp.concatenate(
            [(fr - hr.astype(F32)).astype(BF16), (fi - hi.astype(F32)).astype(BF16)], axis=1
        )
        basis = jnp.concatenate([t_s[0, rows, :].astype(BF16), t_s[1, rows, :].astype(BF16)], axis=1)
        dims = (((0,), (0,)), ((), ()))
        return lax.dot_general(basis, high, dims, preferred_element_type=F32) + lax.dot_general(
            basis, low, dims, preferred_element_type=F32
        )

    gram = jnp.zeros((2 * LANES, 2 * LANES), F32)
    order = sorted(range(1, n_pb), key=lambda v: -min(v, n_pb - v))
    split = share % block == 0
    if not split:
        gram = lax.fori_loop(0, n_blocks, lambda g, acc: acc + inverse_block(g), gram)
    sends = {}
    ring = n_pb == 4

    def rows_of(d):
        return pl.ds(pl.multiple_of(lax.rem(pb + d, n_pb) * share, share), share)

    def ring_copy(slot, to, source, target):
        return pltpu.make_async_remote_copy(
            src_ref=source,
            dst_ref=target,
            send_sem=f_send.at[slot],
            recv_sem=f_recv.at[slot],
            device_id={"ka": ka, "pb": lax.rem(pb + to, n_pb)},
            device_id_type=MESH,
        )

    if ring:
        sides = (1, n_pb - 1)
        relays = [ring_copy(c, sides[c], fbf.at[c, rows_of(2)], rcv.at[2, c]) for c in range(2)]
        early = [ring_copy(2 + i, sides[i], fbf.at[1 - i, rows_of(sides[i])], rcv.at[i, 1 - i]) for i in range(2)]
        late = [ring_copy(4 + i, sides[i], fbf.at[i, rows_of(sides[i])], rcv.at[i, i]) for i in range(2)]
    for d in order + [0]:
        to = lax.rem(pb + d, n_pb)
        if split:
            for g in range(share // block):
                gram = gram + inverse_block(to * (share // block) + g)
        if ring and d == 2:
            for copy in relays:
                copy.start()
        if ring and d in sides:
            early[sides.index(d)].start()
        if d and not ring:
            copy = pltpu.make_async_remote_copy(
                src_ref=fbf.at[:, pl.ds(pl.multiple_of(to * share, share), share), :],
                dst_ref=rcv.at[d - 1],
                send_sem=f_send.at[d - 1],
                recv_sem=f_recv.at[d - 1],
                device_id={"ka": ka, "pb": to},
                device_id_type=MESH,
            )
            if d not in (1, n_pb - 1):
                copy.start()
            sends[d] = copy

    same = gram[:LANES, :LANES] + gram[LANES:, LANES:]
    cross = gram[:LANES, LANES:] - gram[LANES:, :LANES]
    keep = lax.rem(row, L) == lax.rem(lane, L)
    same = jnp.where(keep, same, 0.0)
    cross = jnp.where(keep, cross, 0.0)
    same = same + same.T
    cross = cross - cross.T
    ab = jnp.concatenate(
        [jnp.sum(v[i * L : (i + 1) * L], axis=0, keepdims=True) for v in (same, cross) for i in range(group)],
        axis=0,
    )
    ab_snd[...] = ab
    swaps = {}
    for d in order:
        copy = pltpu.make_async_remote_copy(
            src_ref=ab_snd,
            dst_ref=ab_rcv.at[d - 1],
            send_sem=a_send.at[d - 1],
            recv_sem=a_recv.at[d - 1],
            device_id={"ka": ka, "pb": lax.rem(pb + d, n_pb)},
            device_id_type=MESH,
        )
        copy.start()
        swaps[d] = copy

    if ring:
        for i in range(2):
            relays[i].wait_recv()
            rows = rows_of(sides[i])
            fbf[i, rows, :] = (fld[i, rows, :] + rcv[2, i].astype(F32)).astype(BF16)
            late[i].start()
    for d in order:
        if not ring and d in (1, n_pb - 1):
            sends[d].start()

    for d in order:
        swaps[d].wait_recv()
        ab = ab + ab_rcv[d - 1]
    ab = ab * (-0.5 / (L * L * L))
    n = 2 * group
    sub = lax.broadcasted_iota(jnp.int32, (n, LANES), 0)
    lan = lax.broadcasted_iota(jnp.int32, (n, LANES), 1)
    other = jnp.concatenate([-ab[group:], ab[:group]], axis=0)
    mat = jnp.where(lan == sub + n, 1.0, 0.0).astype(F32)
    for k in range(group):
        a = jnp.sum(jnp.where(lan // L == k, ab, 0.0), axis=1, keepdims=True)
        b = jnp.sum(jnp.where(lan // L == k, other, 0.0), axis=1, keepdims=True)
        mat = jnp.where(lan == k, a, mat)
        mat = jnp.where(lan == group + k, b, mat)
    for k in range(n - 1):
        col = jnp.broadcast_to(mat[:, k : k + 1], (n, LANES))
        ratio = col / col[k : k + 1, :]
        mat = mat - jnp.where(sub > k, ratio, 0.0) * mat[k : k + 1, :]
    diag = jnp.sum(jnp.where(lan == sub, mat, 0.0), axis=1, keepdims=True)
    mat = mat / jnp.sqrt(diag)
    mat_ref[...] = mat

    own = pl.multiple_of(pb * share, share)
    for copy in early + late if ring else [sends[d] for d in order]:
        copy.wait_recv()
    for c in range(2):
        total = fld[c, pl.ds(own, share), :]
        for slot in range(2 if ring else n_pb - 1):
            total = total + rcv[slot, c].astype(F32)
        own_ref[c] = total

    for copy in gathers:
        copy.wait_send()
    for copy in relays + early + late if ring else [sends[d] for d in order]:
        copy.wait_send()
    for d in order:
        swaps[d].wait_send()


def project(mat_ref, own_ref, out_ref):
    L = GRID
    group = LANES // L
    n = 2 * group
    mat = mat_ref[...]
    img = {}
    quarter = own_ref.shape[1] // group
    lane_q = lax.broadcasted_iota(jnp.int32, (quarter, LANES), 1) // L
    for c in range(2):
        rows = [own_ref[c, pl.ds(y, quarter, stride=group), :] for y in range(group)]
        for k in range(group):
            turned = jnp.zeros((quarter, LANES), F32)
            for y in range(group):
                shift = (y - k) % group * L
                moved = pltpu.roll(rows[y], shift, 1) if shift else rows[y]
                turned = jnp.where(lane_q == y, moved, turned)
            img[k, c] = turned

    cols = [jnp.broadcast_to(mat[:, n + k : n + k + 1], (n, LANES)) for k in range(n)]
    for r in range(n):
        w = [col[r : r + 1, :] for col in cols]
        re = jnp.zeros((quarter, LANES), F32)
        im = jnp.zeros((quarter, LANES), F32)
        for k in range(group):
            re = re + w[k] * img[k, 0] - w[group + k] * img[k, 1]
            im = im + w[k] * img[k, 1] + w[group + k] * img[k, 0]
        out_ref[r, pl.ds(0, quarter, stride=2), :] = re
        out_ref[r, pl.ds(1, quarter, stride=2), :] = im


def local(n_ka, n_pb, targets, partners, pair_map, shifts):
    L = GRID
    plane = L * L
    bands = targets.shape[1]
    occ = partners.shape[1]
    share = plane // n_pb
    group = LANES // L

    def interleaved(v):
        v = v.reshape(v.shape[0], 2, -1, LANES).transpose(0, 2, 1, 3)
        return v.reshape(v.shape[0], -1, LANES)

    t = interleaved(targets[0])
    p = interleaved(partners[0])
    consts = tables(L, group)
    vmem = pl.BlockSpec(memory_space=pltpu.VMEM)
    smem = pl.BlockSpec(memory_space=pltpu.SMEM)
    dma = pltpu.SemaphoreType.DMA
    hbm = pl.BlockSpec(memory_space=pltpu.HBM)
    right, left, sel, spread = consts
    own, mat = pl.pallas_call(
        functools.partial(body, n_ka, n_pb),
        out_shape=(
            jax.ShapeDtypeStruct((2, share, LANES), F32),
            jax.ShapeDtypeStruct((2 * bands, LANES), F32),
        ),
        in_specs=[smem, smem, vmem] + [hbm] * 5,
        out_specs=(vmem, vmem),
        scratch_shapes=[
            pltpu.VMEM(t.shape, BF16),
            pltpu.VMEM(sel.shape, BF16),
            pltpu.VMEM(spread.shape, BF16),
            pltpu.VMEM(right.shape, BF16),
            pltpu.VMEM(left.shape, BF16),
            dma((5,)),
            pltpu.VMEM((n_ka,) + p.shape, BF16),
            pltpu.VMEM(t.shape, F32),
            pltpu.VMEM(p.shape, F32),
            pltpu.VMEM((2, plane, LANES), F32),
            pltpu.VMEM((occ, 2, plane, LANES), F32),
            pltpu.VMEM((2, occ, plane, LANES), BF16),
            pltpu.VMEM((2, plane, LANES), F32),
            pltpu.VMEM((2, plane, LANES), BF16),
            pltpu.VMEM((n_pb - 1, 2, share, LANES), BF16),
            pltpu.VMEM((2 * bands, LANES), F32),
            pltpu.VMEM((n_pb - 1, 2 * bands, LANES), F32),
            dma((n_ka - 1,)),
            dma((n_ka - 1,)),
            dma((2 * n_pb,)),
            dma((2 * n_pb,)),
            dma((n_pb - 1,)),
            dma((n_pb - 1,)),
        ],
        compiler_params=pltpu.CompilerParams(collective_id=0, has_side_effects=True),
    )(pair_map, shifts[0], p, t, sel, spread, right, left)
    steps = 2
    out = pl.pallas_call(
        project,
        grid=(steps,),
        out_shape=jax.ShapeDtypeStruct((2 * bands, 2 * share // group, LANES), F32),
        in_specs=[
            pl.BlockSpec((2 * bands, LANES), lambda i: (0, 0)),
            pl.BlockSpec((2, share // steps, LANES), lambda i: (0, i, 0)),
        ],
        out_specs=pl.BlockSpec((2 * bands, 2 * share // group // steps, LANES), lambda i: (0, i, 0)),
    )(mat, own)
    out = out.reshape(2 * bands, share // group, 2, LANES).transpose(0, 2, 1, 3)
    return out.reshape(1, 2 * bands, 2, share * L)


def solution(mesh):
    return jax.shard_map(
        functools.partial(local, mesh.shape["ka"], mesh.shape["pb"]),
        mesh=mesh,
        in_specs=(
            P("ka", None, None, None),
            P("pb", None, None, "ka"),
            P("ka", "pb"),
            P("ka", "pb", None),
        ),
        out_specs=P("ka", None, None, "pb"),
        check_vma=False,
    )
```
